32 devices in a mesh: samp: 8 (over y, x, core), exp: 4 (over z).
Axes of the slice: x: 2, y: 2, z: 4, core: 2. Of those that a mesh axis runs over, the one named last changes fastest.
Arguments:
- prompt_states: bfloat16 [4, 8, 64, 2048], P('exp', 'samp'), may hold values from -6 to 6
- edit_offsets: bfloat16 [1, 4, 8, 64, 2048], P(None, 'exp', 'samp'), may hold values from -6 to 6
- targets: bfloat16 [2, 4, 8, 64, 2048], P(None, 'exp', 'samp'), may hold values from -6 to 6
- router: bfloat16 [2048, 32], replicated, may hold values from -0.125 to 0.125
- route_ids: int32 [2, 4, 8, 64, 8], P(None, 'exp', 'samp'), may hold values from 0 to 31, all different within a row; in each aligned block of 64 rows (0 to 63, 64 to 127, ..., all dimensions but the last counted through in order) at most 20 rows name the same one
- chosen: int32 [1, 4], replicated, may hold values from 0 to 7
- lengths: int32 [2, 4, 8], P(None, 'exp', 'samp'), may hold values from 16 to 64, as said below
- w_gate: bfloat16 [32, 2048, 768], P(('samp', 'exp')), may hold values from -0.125 to 0.125
- w_up: bfloat16 [32, 2048, 768], P(('samp', 'exp')), may hold values from -0.125 to 0.125
- w_down: bfloat16 [32, 768, 2048], P(('samp', 'exp')), may hold values from -0.21875 to 0.21875
Outputs:
- grad_gate: bfloat16 [32, 2048, 768], P(('samp', 'exp'))
- grad_up: bfloat16 [32, 2048, 768], P(('samp', 'exp'))
- grad_down: bfloat16 [32, 768, 2048], P(('samp', 'exp'))
- advantages: float32 [2, 4, 8], P(None, 'exp', 'samp')
The draws below stay inside these ranges and needn't reach their ends.
Inputs may be any that keep to these rules, and one draw needn't show every extreme that they name: `route_ids`: in each block of 64 rows that one repair has in one round, the 8 ids of a row differ, no expert is named by more than 20 rows, a bound that some block reaches. `lengths`: in each round and prompt some sample has exactly 64 scored tokens.
All inputs are finite; a program needn't handle non-finite values.
Results may differ from the reference program's by a relative error of at most 0.015.
Values may be sent and summed in bfloat16 or wider, within the bound.
A program may use at most 128 MiB of HBM per device.

```python
import math
import jax
import jax.numpy as jnp
import numpy as np
from jax import lax

D = 2048
FF = 768
TOP = 8
SEQ = 64
ROUNDS = 2
SAMPLES = 8
GROUPS = 4
EXPERTS = 32
CAP = 20


def draw_lengths(key, part):
    first_key, second_key = jax.random.split(jax.random.fold_in(key, 11))
    drawn = jax.random.randint(first_key, (ROUNDS, GROUPS, SAMPLES), SEQ // 4, SEQ + 1)
    longest = jax.random.randint(second_key, (ROUNDS, GROUPS, 1), 0, SAMPLES)
    sample_iota = jnp.arange(SAMPLES, dtype=jnp.int32)[None, None, :]
    return jnp.where(sample_iota == longest, SEQ, drawn).astype(jnp.int32)


def place_ends(values, key, low, largest):
    place = [jax.random.randint(jax.random.fold_in(key, axis), (), 0, length) for axis, length in enumerate(values.shape)]
    widest = values.shape.index(max(values.shape))
    neighbour = place[:widest] + [(place[widest] + 1) % values.shape[widest]] + place[widest + 1:]
    return values.at[tuple(place)].set(low).at[tuple(neighbour)].set(largest)


def block_levels(rng, dims, cuts, low, top_value):
    def one(dim, shards_of):
        steps = jax.random.uniform(jax.random.fold_in(jax.random.fold_in(rng, 6), dim), (shards_of,), jnp.float32, low / len(cuts), top_value / len(cuts))
        return jnp.repeat(jnp.exp(steps), dims[dim] // shards_of).reshape((-1,) + (1,) * (len(dims) - dim - 1))

    gain = one(*cuts[0])
    for cut in cuts[1:]:
        gain = gain * one(*cut)
    return gain


def routed_block(stream_key, own, number, rows, amount, top, reach, skew):
    order = jax.random.permutation(stream_key, amount)
    crowded, ordinary = load_shares(amount, rows * top, reach, skew, True), load_shares(amount, rows * top, reach, skew, False)
    places = jnp.arange(amount)

    def named(sizes, rotation):
        used = int((sizes > 0).sum())
        fixed = max(1, used // 4)
        moved = fixed + (places - fixed + rotation * (used - fixed)) % max(1, amount - fixed)
        return jnp.zeros((amount,), jnp.int32).at[order[jnp.where(places < fixed, places, moved)]].set(jnp.asarray(sizes, jnp.int32))

    sizes = jnp.where(number % 4 == 0, named(crowded, number // 4), named(ordinary, number - number // 4 - 1))
    mixed = jax.random.permutation(jax.random.fold_in(own, 3), amount)
    source_of, receiver = mixed[0:amount // 2 * 2:2], mixed[1:amount // 2 * 2:2]
    room = jnp.minimum(sizes[source_of] - 1, reach - sizes[receiver]) // 2
    room = jnp.where((source_of == order[0]) | (receiver == order[0]) | (sizes[receiver] == 0), 0, jnp.maximum(room, 0))
    moved = jax.random.randint(jax.random.fold_in(own, 4), (amount // 2,), 0, 1 << 20) % (room + 1)
    sizes = sizes.at[source_of].add(-moved).at[receiver].add(moved)
    items = jnp.searchsorted(jnp.cumsum(sizes), jnp.arange(rows * top), side="right").astype(jnp.int32)
    grid = items.reshape(top, rows).T
    grid = grid[jax.random.permutation(jax.random.fold_in(own, 1), rows)]
    rotation = jax.random.randint(jax.random.fold_in(own, 2), (rows, 1), 0, top)
    return jnp.take_along_axis(grid, (jnp.arange(top)[None, :] + rotation) % top, axis=1)


def load_shares(amount, total, limit, skew, full):
    loads = [(1 << 20) // math.isqrt(grade ** skew) + 1 for grade in range(1, amount + 1)]
    largest = limit if full else min(limit, max(-(-total // amount), total * loads[0] // sum(loads)))
    least = 1 if total - largest >= amount - 1 else 0
    counts, surplus = [largest] + [least] * (amount - 1), total - largest - least * (amount - 1)
    while surplus > 0:
        candidates = [i for i in range(1, amount) if counts[i] < largest] or [i for i in range(1, amount) if counts[i] < limit]
        mass, left = sum([loads[i] for i in candidates]), surplus
        for i in candidates:
            extra = min(limit - counts[i], max(1, left * loads[i] // mass), surplus)
            counts[i] = counts[i] + extra
            surplus = surplus - extra
    return np.array(counts)


def bell_draw(key, extent, deviation, limit, pieces=(), kind=jnp.bfloat16):
    loudness = block_levels(key, extent, pieces, -0.22, 0.18) if pieces else 1.0
    array = jax.random.normal(key, extent, jnp.float32) * deviation * loudness
    return jnp.minimum(jnp.maximum(array, -limit), limit).astype(kind)


def setup_inputs(seed: int = 0) -> dict:
    streams_of = jax.random.split(jax.random.key(seed), 11)
    prompt_states = bell_draw(streams_of[0], (GROUPS, SAMPLES, SEQ, D), 1.0, 6.0, ((0, 4), (1, 8)))
    edit_offsets = bell_draw(streams_of[1], (ROUNDS - 1, GROUPS, SAMPLES, SEQ, D), 1.0, 6.0, ((1, 4), (2, 8)))
    targets = bell_draw(streams_of[2], (ROUNDS, GROUPS, SAMPLES, SEQ, D), 1.0, 6.0, ((1, 4), (2, 8)))
    router = bell_draw(streams_of[3], (D, EXPERTS), D ** -0.5, 0.125)
    route_ids_keys = jax.random.split(jax.random.fold_in(streams_of[4], 1), ROUNDS * GROUPS * SAMPLES * SEQ // SEQ)
    route_ids_turns = jax.random.permutation(jax.random.fold_in(streams_of[4], 3), ROUNDS * GROUPS * SAMPLES * SEQ // SEQ)
    route_ids = jax.vmap(lambda own, number: routed_block(jax.random.fold_in(streams_of[4], 2), own, number, SEQ, EXPERTS, TOP, CAP, 1))(route_ids_keys, route_ids_turns).reshape((ROUNDS, GROUPS, SAMPLES, SEQ, TOP))
    chosen = place_ends(jax.random.randint(streams_of[5], (ROUNDS - 1, GROUPS), 0, SAMPLES), jax.random.fold_in(streams_of[5], 1), 0, SAMPLES - 1).astype(jnp.int32)
    lengths = draw_lengths(jax.random.fold_in(streams_of[10], 71), 0)
    w_gate = bell_draw(streams_of[7], (EXPERTS, D, FF), D ** -0.5, 0.125, ((0, 32),))
    w_up = bell_draw(streams_of[8], (EXPERTS, D, FF), D ** -0.5, 0.125, ((0, 32),))
    w_down = bell_draw(streams_of[9], (EXPERTS, FF, D), FF ** -0.5, 0.21875, ((0, 32),))
    return {"prompt_states": prompt_states, "edit_offsets": edit_offsets, "targets": targets, "router": router, "route_ids": route_ids, "chosen": chosen, "lengths": lengths, "w_gate": w_gate, "w_up": w_up, "w_down": w_down}


def expert_pass(expert_rows, gate_weight, up_weight, down_weight):
    pre_gate = jnp.dot(expert_rows, gate_weight, preferred_element_type=jnp.float32)
    pre_up = jnp.dot(expert_rows, up_weight, preferred_element_type=jnp.float32)
    hidden = (jax.nn.silu(pre_gate) * pre_up).astype(jnp.bfloat16)
    result = jnp.dot(hidden, down_weight, preferred_element_type=jnp.float32).astype(jnp.bfloat16)
    return (pre_gate, pre_up, hidden, result)

def build_table(route_now):
    flat_ids = route_now.reshape(GROUPS, SAMPLES, SEQ * TOP)
    onehot = (flat_ids[..., None] == jnp.arange(EXPERTS, dtype=jnp.int32)).astype(jnp.int32)
    slot_index = lax.optimization_barrier(jnp.sum(jnp.cumsum(onehot, axis=2) * onehot, axis=3)) - 1
    source = jnp.arange(SAMPLES, dtype=jnp.int32)[None, :, None] * GROUPS + jnp.arange(GROUPS, dtype=jnp.int32)[:, None, None]
    position = (source * CAP + slot_index).astype(jnp.int32)
    pair_index = jnp.arange(GROUPS * SAMPLES * SEQ * TOP, dtype=jnp.int32).reshape(GROUPS, SAMPLES, SEQ * TOP)
    empty_pair = GROUPS * SAMPLES * SEQ * TOP
    pair_table = jnp.full((EXPERTS, GROUPS * SAMPLES * CAP), empty_pair, dtype=jnp.int32)
    return pair_table.at[flat_ids, position].set(pair_index)

def padded(values, width_tail):
    return jnp.concatenate([values, jnp.zeros((1,) + width_tail, values.dtype)], axis=0)

def forward_round(tokens_now, route_now, router, w_gate, w_up, w_down):
    token_count = GROUPS * SAMPLES * SEQ
    token_flat = tokens_now.reshape(token_count, D)
    logits = jnp.dot(token_flat, router, preferred_element_type=jnp.float32).reshape(GROUPS, SAMPLES, SEQ, EXPERTS)
    picked = jnp.take_along_axis(logits, route_now, axis=3)
    sigmoid_values = jax.nn.sigmoid(picked)
    gate_values = (sigmoid_values / lax.optimization_barrier(jnp.sum(sigmoid_values, axis=3, keepdims=True))).astype(jnp.bfloat16)
    pair_table = build_table(route_now)
    token_pad = padded(token_flat, (D,))
    gate_pad = padded(gate_values.reshape(token_count * TOP).astype(jnp.float32), ())

    def step_fn(summed, inputs):
        pair_ids, gate_weight, up_weight, down_weight = inputs
        row_ids = pair_ids // TOP
        unused_a, unused_b, unused_c, result = expert_pass(token_pad[row_ids], gate_weight, up_weight, down_weight)
        return (summed.at[row_ids].add(gate_pad[pair_ids][:, None] * result.astype(jnp.float32)), None)
    summed, unused = lax.scan(step_fn, jnp.zeros((token_count + 1, D), jnp.float32), (pair_table, w_gate, w_up, w_down))
    mixed_sum = token_flat.astype(jnp.float32) + summed[:token_count]
    mixed_rows = mixed_sum.astype(jnp.bfloat16)
    return (mixed_sum.reshape(GROUPS, SAMPLES, SEQ, D), mixed_rows.reshape(GROUPS, SAMPLES, SEQ, D), gate_values, pair_table)

def reference(prompt_states, edit_offsets, targets, router, route_ids, chosen, lengths, w_gate, w_up, w_down):
    token_count = GROUPS * SAMPLES * SEQ
    tokens_now = prompt_states
    tables_all = []
    token_pads = []
    target_pads = []
    coef_pads = []
    advantage_list = []
    positions = jnp.arange(SEQ, dtype=jnp.int32)
    for turn_index in range(ROUNDS):
        mixed_sum, mixed_rows, gate_values, pair_table = forward_round(tokens_now, route_ids[turn_index], router, w_gate, w_up, w_down)
        scores = lax.optimization_barrier(jnp.sum(mixed_sum * targets[turn_index].astype(jnp.float32), axis=3)) / math.sqrt(D)
        valid_mask = (positions[None, None, :] < lengths[turn_index][..., None]).astype(jnp.float32)
        reward = lax.optimization_barrier(jnp.sum(valid_mask * scores, axis=2)) / lengths[turn_index].astype(jnp.float32)
        advantage = reward - lax.optimization_barrier(jnp.mean(reward, axis=1, keepdims=True))
        coef = (advantage[..., None, None] * valid_mask[..., None] * gate_values.astype(jnp.float32)).astype(jnp.bfloat16)
        tables_all.append(pair_table)
        token_pads.append(padded(tokens_now.reshape(token_count, D), (D,)))
        target_pads.append(padded(targets[turn_index].reshape(token_count, D), (D,)))
        coef_pads.append(padded(coef.reshape(token_count * TOP), ()))
        advantage_list.append(advantage)
        if turn_index + 1 < ROUNDS:
            best_rows = mixed_rows[jnp.arange(GROUPS, dtype=jnp.int32), chosen[turn_index]]
            tokens_now = (best_rows[:, None].astype(jnp.float32) + edit_offsets[turn_index].astype(jnp.float32)).astype(jnp.bfloat16)
    stacked_tables = jnp.stack(tables_all, axis=1)

    def grad_step(carry, inputs):
        table_rounds, gate_weight, up_weight, down_weight = inputs
        grad_gate = jnp.zeros((D, FF), jnp.float32)
        grad_up = jnp.zeros((D, FF), jnp.float32)
        grad_down = jnp.zeros((FF, D), jnp.float32)
        for turn_index in range(ROUNDS):
            pair_ids = table_rounds[turn_index]
            row_ids = pair_ids // TOP
            expert_rows = token_pads[turn_index][row_ids]
            pre_gate, pre_up, hidden, unused = expert_pass(expert_rows, gate_weight, up_weight, down_weight)
            cotangent = (coef_pads[turn_index][pair_ids].astype(jnp.float32)[:, None] * target_pads[turn_index][row_ids].astype(jnp.float32)).astype(jnp.bfloat16)
            grad_down = grad_down + jnp.dot(hidden.T, cotangent, preferred_element_type=jnp.float32)
            hidden_grad = jnp.dot(cotangent, down_weight.T, preferred_element_type=jnp.float32)
            sigmoid_gate = jax.nn.sigmoid(pre_gate)
            gate_grad = (hidden_grad * pre_up * sigmoid_gate * (1.0 + pre_gate * (1.0 - sigmoid_gate))).astype(jnp.bfloat16)
            up_grad = (hidden_grad * pre_gate * sigmoid_gate).astype(jnp.bfloat16)
            grad_gate = grad_gate + jnp.dot(expert_rows.T, gate_grad, preferred_element_type=jnp.float32)
            grad_up = grad_up + jnp.dot(expert_rows.T, up_grad, preferred_element_type=jnp.float32)
        return (carry, (grad_gate.astype(jnp.bfloat16), grad_up.astype(jnp.bfloat16), grad_down.astype(jnp.bfloat16)))
    unused, grads = lax.scan(grad_step, jnp.zeros((), jnp.float32), (stacked_tables, w_gate, w_up, w_down))
    return (grads[0], grads[1], grads[2], jnp.stack(advantage_list))
```

```python
import math

import jax
import jax.numpy as jnp
from jax import lax
from jax.sharding import PartitionSpec as P

BOTH = ("samp", "exp")
F32 = jnp.float32
BF16 = jnp.bfloat16


def dot(a, b):
    return jnp.dot(a, b, preferred_element_type=F32)


def dot_tn(a, b):
    return lax.dot_general(a, b, (((0,), (0,)), ((), ())), preferred_element_type=F32)


def dot_nt(a, b):
    return lax.dot_general(a, b, (((1,), (1,)), ((), ())), preferred_element_type=F32)


def per_device(
    prompt_states, edit_offsets, targets, router, route_ids, chosen, lengths, w_gate, w_up, w_down
):
    seq = prompt_states.shape[2]
    width = prompt_states.shape[3]
    rounds = route_ids.shape[0]
    top = route_ids.shape[4]
    experts = router.shape[1]
    cap = seq * top * 5 // (4 * experts)
    samplers = lax.axis_size("samp")
    groups = lax.axis_size("exp")
    my_samp = lax.axis_index("samp")
    my_group = lax.axis_index("exp")
    my_expert = my_samp * groups + my_group
    block = groups * cap
    rows = samplers * block
    tokens = groups * seq
    gate_weight, up_weight, down_weight = w_gate[0], w_up[0], w_down[0]
    meta_width = -(-(experts + 4) // 128) * 128
    expert_iota = jnp.arange(experts, dtype=jnp.int32)
    positions = jnp.arange(seq, dtype=jnp.int32)

    row_iota = jnp.arange(rows, dtype=jnp.int32)
    row_samp = row_iota // block
    row_group = (row_iota % block) // cap
    row_repair = row_samp * groups + row_group
    repair_onehot = row_repair[:, None] == jnp.arange(samplers * groups, dtype=jnp.int32)[None, :]
    token_iota = jnp.arange(tokens, dtype=jnp.int32)
    tril = (positions[:, None] <= positions[None, :]).astype(BF16)

    def meta_of(r):
        mask = jnp.any(route_ids[r, 0, 0][:, :, None] == expert_iota[None, None, :], axis=1)
        length = lengths[r, 0, 0]
        cols = jnp.stack(
            [
                positions.astype(BF16),
                (positions < length).astype(BF16),
                jnp.broadcast_to(length.astype(BF16), (seq,)),
                jnp.ones((seq,), BF16),
            ],
            axis=1,
        )
        pad = jnp.zeros((seq, meta_width - experts - 4), BF16)
        return jnp.concatenate([mask.astype(BF16), cols, pad], axis=1)

    def over_exp(block_rows):
        return lax.all_gather(block_rows, "exp", axis=0, tiled=True)

    def placing_of(meta):
        mine = (
            jnp.arange(experts, dtype=jnp.int32)[None, :]
            == jnp.arange(samplers, dtype=jnp.int32)[:, None] * groups + my_group
        ).astype(BF16)
        picked = dot_nt(mine, meta[:, :experts]).astype(BF16)
        picked = picked.reshape(samplers * groups, seq)
        rank = dot(picked, tril).astype(jnp.int32).reshape(samplers, tokens) - 1
        code = jnp.where(
            picked.reshape(samplers, tokens) > 0.5, (token_iota // seq)[None, :] * cap + rank, -1
        )
        slots = jnp.arange(block, dtype=jnp.int32)
        return (code[:, None, :] == slots[None, :, None]).astype(BF16).reshape(rows, tokens)

    def to_experts(placing, values):
        placed = dot(placing, values).astype(BF16)
        return lax.all_to_all(placed, "samp", split_axis=0, concat_axis=0, tiled=True)

    def columns_of(meta):
        info = meta[:, experts : experts + 4].astype(F32)
        used = info[:, 3] > 0.5
        return meta[:, :experts] > 0.5, info[:, 0].astype(jnp.int32), info[:, 1], info[:, 2], used

    def gates_of(received, mask, used):
        logits = dot(received, router)
        sig = jnp.where(mask, jax.nn.sigmoid(logits), 0.0)
        total = jnp.where(used, jnp.sum(sig, axis=1), 1.0)
        own = jnp.sum(jnp.where(expert_iota[None, :] == my_expert, sig, 0.0), axis=1)
        return (own / total).astype(BF16)

    def own_part(x, target, r):
        length = lengths[r, 0, 0]
        valid = (positions < length).astype(F32)
        score = jnp.sum(x.astype(F32) * target.astype(F32), axis=1) / math.sqrt(width)
        return jnp.sum(valid * score) / length.astype(F32)

    def reward_part(hidden, back, gate, valid, length, used, own):
        score = jnp.sum(hidden.astype(F32) * back, axis=1) / math.sqrt(width)
        score = gate.astype(F32) * valid * score / jnp.where(used, length, 1.0)
        part = jnp.sum(jnp.where(repair_onehot, score[:, None], 0.0), axis=0)
        repairs = jnp.arange(samplers * groups, dtype=jnp.int32)
        return part + jnp.where(repairs == my_expert, own, 0.0)

    metas = [meta_of(r) for r in range(rounds)]
    bases = [prompt_states[0, 0]] + [edit_offsets[r, 0, 0] for r in range(rounds - 1)]
    parts = []
    saved = []
    mixed = None
    for r in range(rounds):
        gathered = over_exp(jnp.concatenate([bases[r], metas[r]], axis=1))
        targets_all = over_exp(targets[r, 0, 0])
        placing = placing_of(gathered[:, width:])
        arrived = to_experts(placing, gathered)
        mask, row_pos, valid, length, used = columns_of(arrived[:, width:])
        received = arrived[:, :width]
        token_code = jnp.where(used, row_group * seq + row_pos, -1)
        own_x = bases[r]
        if r > 0:
            lift = (token_code[:, None] == token_iota[None, :]).astype(BF16)
            received = (dot(lift, mixed) + received.astype(F32)).astype(BF16)
            best = lax.dynamic_slice_in_dim(mixed, my_group * seq, seq, axis=0)
            own_x = (best.astype(F32) + own_x.astype(F32)).astype(BF16)
        gate = gates_of(received, mask, used)
        pre_gate = dot(received, gate_weight)
        pre_up = dot(received, up_weight)
        hidden = (jax.nn.silu(pre_gate) * pre_up).astype(BF16)
        if r + 1 < rounds:
            choice = chosen[r]
            row_choice = jnp.sum(
                jnp.where(
                    row_group[:, None] == jnp.arange(groups, dtype=jnp.int32)[None, :],
                    choice[None, :],
                    0,
                ),
                axis=1,
            )
            keep = row_samp == row_choice
            slot_code = jnp.where(keep, row_iota % block, -1)
            slots = jnp.arange(block, dtype=jnp.int32)
            take = (slot_code[None, :] == slots[:, None]).astype(BF16)
            result = dot(dot(take, hidden).astype(BF16), down_weight).astype(BF16)
            spread = jnp.where(
                (jnp.where(keep, token_code, -1)[:, None] == token_iota[None, :]),
                gate[:, None],
                jnp.zeros((), BF16),
            )
            combine = dot(take, spread).astype(BF16)
            start = (choice[token_iota // seq] == my_samp) & (token_iota // seq == my_group)
            part = dot_tn(combine, result) + jnp.where(
                start[:, None], gathered[:, :width].astype(F32), 0.0
            )
            pieces = lax.all_to_all(
                part.astype(BF16), BOTH, split_axis=0, concat_axis=0, tiled=True
            )
            pieces = pieces.reshape(samplers * groups, -1, width)
            summed = jnp.sum(pieces.astype(F32), axis=0).astype(BF16)
            mixed = lax.all_gather(summed, BOTH, axis=0, tiled=True)
        target_rows = to_experts(placing, targets_all)
        back = dot_nt(target_rows, down_weight)
        parts.append(
            reward_part(
                hidden, back, gate, valid, length, used, own_part(own_x, targets[r, 0, 0], r)
            )
        )
        saved.append((received, target_rows, gate, valid, pre_gate, pre_up, hidden, back))
    rewards = lax.psum(jnp.stack(parts), BOTH).reshape(rounds, samplers, groups)
    advantage = rewards - jnp.mean(rewards, axis=1, keepdims=True)
    flat = advantage.reshape(rounds, samplers * groups)
    grad_gate = grad_up = grad_down = 0.0
    for r, (received, target_rows, gate, valid, pre_gate, pre_up, hidden, back) in enumerate(saved):
        row_adv = jnp.sum(jnp.where(repair_onehot, flat[r][None, :], 0.0), axis=1)
        coef = (row_adv * valid * gate.astype(F32)).astype(BF16).astype(F32)[:, None]
        hidden_grad = coef * back
        sg = jax.nn.sigmoid(pre_gate)
        gate_grad = (hidden_grad * pre_up * sg * (1.0 + pre_gate * (1.0 - sg))).astype(BF16)
        up_grad = (hidden_grad * pre_gate * sg).astype(BF16)
        weighted = (hidden.astype(F32) * coef).astype(BF16)
        grad_down = grad_down + dot_tn(weighted, target_rows)
        grad_gate = grad_gate + dot_tn(received, gate_grad)
        grad_up = grad_up + dot_tn(received, up_grad)
    repairs = jnp.arange(samplers * groups, dtype=jnp.int32)
    my_adv = jnp.sum(jnp.where(repairs[None, :] == my_expert, flat, 0.0), axis=1)
    return (
        grad_gate.astype(BF16)[None],
        grad_up.astype(BF16)[None],
        grad_down.astype(BF16)[None],
        my_adv.reshape(rounds, 1, 1),
    )


def solution(mesh):
    placed = (
        P("exp", "samp", None, None),
        P(None, "exp", "samp", None, None),
        P(None, "exp", "samp", None, None),
        P(),
        P(None, "exp", "samp", None, None),
        P(),
        P(None, "exp", "samp"),
        P(("samp", "exp"), None, None),
        P(("samp", "exp"), None, None),
        P(("samp", "exp"), None, None),
    )
    return jax.shard_map(
        per_device,
        mesh=mesh,
        in_specs=placed,
        out_specs=(
            P(("samp", "exp"), None, None),
            P(("samp", "exp"), None, None),
            P(("samp", "exp"), None, None),
            P(None, "exp", "samp"),
        ),
        check_vma=False,
    )
```

```python
import functools
import math

import jax
import jax.numpy as jnp
from jax import lax
from jax.experimental import pallas as pl
from jax.experimental.pallas import tpu as pltpu
from jax.sharding import PartitionSpec as P

F32 = jnp.float32
BF16 = jnp.bfloat16


def dot(a, b):
    return jnp.dot(a, b, preferred_element_type=F32)


def dot_tn(a, b):
    return lax.dot_general(a, b, (((0,), (0,)), ((), ())), preferred_element_type=F32)


def dot_nt(a, b):
    return lax.dot_general(a, b, (((1,), (1,)), ((), ())), preferred_element_type=F32)


MESH = pl.DeviceIdType.MESH
VMEM = pl.BlockSpec(memory_space=pltpu.VMEM)
ANY = pl.BlockSpec(memory_space=pl.ANY)


def greet(peers):
    barrier = pltpu.get_barrier_semaphore()
    for peer in peers:
        pl.semaphore_signal(barrier, inc=1, device_id=peer, device_id_type=MESH)
    pl.semaphore_wait(barrier, len(peers))


def remote(src, dst, send, recv, peer):
    return pltpu.make_async_remote_copy(
        src_ref=src, dst_ref=dst, send_sem=send, recv_sem=recv, device_id=peer, device_id_type=MESH
    )


def dispatch_kernel(ns, ng, seq, block, rounds, *refs):
    count = 2 * rounds
    code_ref, ins, outs = refs[0], refs[1 : 1 + count], refs[1 + count : 1 + 2 * count]
    rest = refs[1 + 2 * count :]
    codes, alls, sends = rest[0], rest[1 : 1 + count], rest[1 + count : 1 + 2 * count]
    place, gs, gr, ss, sr, own_sem = rest[1 + 2 * count :]
    me_s, me_g = lax.axis_index("samp"), lax.axis_index("exp")
    exp_peers = [(me_s, lax.rem(me_g + k, ng)) for k in range(1, ng)]
    samp_peers = [(lax.rem(me_s + k, ns), me_g) for k in range(1, ns)]
    greet(exp_peers + samp_peers)
    mine = pl.ds(pl.multiple_of(me_g * seq, seq), seq)
    code_copies = []
    for k, peer in enumerate(exp_peers):
        copy = remote(
            code_ref.at[peer[1]], codes.at[me_g], gs.at[count, k], gr.at[count, k], peer
        )
        copy.start()
        code_copies.append(copy)
    copies = []
    for i in range(count):
        here = []
        for k, peer in enumerate(exp_peers):
            copy = remote(ins[i], alls[i].at[mine, :], gs.at[i, k], gr.at[i, k], peer)
            copy.start()
            here.append(copy)
        copies.append(here)
    codes[me_g] = code_ref[me_g]
    for i in range(count):
        alls[i][mine, :] = ins[i][...]
    for copy in code_copies:
        copy.wait()
    slots = lax.broadcasted_iota(jnp.int32, (block, ng * seq), 0).astype(F32)
    for r in range(rounds):
        line = jnp.concatenate([codes[g][:, r * seq : (r + 1) * seq] for g in range(ng)], axis=1)
        for d in range(ns):
            hit = jnp.where(line[d : d + 1, :] == slots, 1.0, 0.0)
            place[r, d * block : (d + 1) * block, :] = hit.astype(BF16)
    home = pl.ds(pl.multiple_of(me_s * block, block), block)
    for i in range(count):
        for copy in copies[i]:
            copy.wait()

        def put(d, i=i):
            part = pl.ds(pl.multiple_of(d * block, block), block)
            sends[i][part, :] = dot(place[i // 2, part, :], alls[i][...]).astype(BF16)
            return part

        def step(k, carry, i=i, put=put):
            d = lax.rem(me_s + k, ns)
            part = put(d)
            remote(
                sends[i].at[part, :], outs[i].at[home, :], ss.at[i, k], sr.at[i, k], (d, me_g)
            ).start()
            return carry

        lax.fori_loop(1, ns, step, 0)
        put(me_s)
        pltpu.make_async_copy(sends[i].at[home, :], outs[i].at[home, :], own_sem.at[i]).start()
    for i in range(count):

        def finish(k, carry, i=i):
            d = lax.rem(me_s + k, ns)
            part = pl.ds(pl.multiple_of(d * block, block), block)
            remote(
                sends[i].at[part, :], outs[i].at[home, :], ss.at[i, k], sr.at[i, k], (d, me_g)
            ).wait()
            return carry

        lax.fori_loop(1, ns, finish, 0)
        pltpu.make_async_copy(sends[i].at[home, :], outs[i].at[home, :], own_sem.at[i]).wait()


def dispatch(code, arrays, ns, ng, seq, block, rounds):
    count = len(arrays)
    widths = [a.shape[1] for a in arrays]
    return pl.pallas_call(
        functools.partial(dispatch_kernel, ns, ng, seq, block, rounds),
        out_shape=[jax.ShapeDtypeStruct((ns * block, w), BF16) for w in widths],
        in_specs=[VMEM] * (1 + count),
        out_specs=[ANY] * count,
        scratch_shapes=[pltpu.VMEM(code.shape, F32)]
        + [pltpu.VMEM((ng * seq, w), BF16) for w in widths]
        + [pltpu.VMEM((ns * block, w), BF16) for w in widths]
        + [
            pltpu.VMEM((rounds, ns * block, ng * seq), BF16),
            pltpu.SemaphoreType.DMA((count + 1, ng - 1)),
            pltpu.SemaphoreType.DMA((count + 1, ng - 1)),
            pltpu.SemaphoreType.DMA((count, ns)),
            pltpu.SemaphoreType.DMA((count, ns)),
            pltpu.SemaphoreType.DMA((count,)),
        ],
        compiler_params=pltpu.CompilerParams(
            collective_id=0, has_side_effects=True, vmem_limit_bytes=48 * 2**20
        ),
    )(code, *arrays)


def mix_kernel(ns, ng, part_ref, out_ref, rows_in, half, cols_in, final, sems_a, sems_b):
    me_s, me_g = lax.axis_index("samp"), lax.axis_index("exp")
    exp_peers = [(me_s, lax.rem(me_g + k, ng)) for k in range(1, ng)]
    samp_peers = [(lax.rem(me_s + k, ns), me_g) for k in range(1, ns)]
    greet(exp_peers + samp_peers)
    high, width = rows_in.shape[1], rows_in.shape[2]
    wide = width // ng

    def rows_of(d):
        return pl.ds(pl.multiple_of(d * high, high), high)

    def cols_of(g):
        return pl.ds(pl.multiple_of(g * wide, wide), wide)

    copies = []
    for k, peer in enumerate(samp_peers):
        copy = remote(
            part_ref.at[rows_of(peer[0]), :],
            rows_in.at[k],
            sems_a.at[0, k],
            sems_a.at[1, k],
            peer,
        )
        copy.start()
        copies.append(copy)
    half[...] = part_ref[rows_of(me_s), :].astype(F32)
    for k, copy in enumerate(copies):
        copy.wait()
        half[...] += rows_in[k].astype(F32)
    copies = []
    for k, peer in enumerate(exp_peers):
        copy = remote(
            half.at[:, cols_of(peer[1])], cols_in.at[k], sems_b.at[0, k], sems_b.at[1, k], peer
        )
        copy.start()
        copies.append(copy)
    total = half[:, cols_of(me_g)]
    for k, copy in enumerate(copies):
        copy.wait()
        total = total + cols_in[k]
    final[...] = total.astype(BF16)
    out_ref[rows_of(me_s), cols_of(me_g)] = final[...]
    copies = []
    for k, peer in enumerate(exp_peers):
        copy = remote(
            final,
            out_ref.at[rows_of(me_s), cols_of(me_g)],
            sems_b.at[2, k],
            sems_b.at[3, k],
            peer,
        )
        copy.start()
        copies.append(copy)
    for copy in copies:
        copy.wait()
    copies = []
    for k, peer in enumerate(samp_peers):
        copy = remote(
            out_ref.at[rows_of(me_s), :],
            out_ref.at[rows_of(me_s), :],
            sems_a.at[2, k],
            sems_a.at[3, k],
            peer,
        )
        copy.start()
        copies.append(copy)
    for copy in copies:
        copy.wait()


def mix(part, ns, ng):
    tokens, width = part.shape
    high = tokens // ns
    return pl.pallas_call(
        functools.partial(mix_kernel, ns, ng),
        out_shape=jax.ShapeDtypeStruct(part.shape, BF16),
        in_specs=[VMEM],
        out_specs=VMEM,
        scratch_shapes=[
            pltpu.VMEM((ns - 1, high, width), BF16),
            pltpu.VMEM((high, width), F32),
            pltpu.VMEM((ng - 1, high, width // ng), F32),
            pltpu.VMEM((high, width // ng), BF16),
            pltpu.SemaphoreType.DMA((4, ns - 1)),
            pltpu.SemaphoreType.DMA((4, ng - 1)),
        ],
        compiler_params=pltpu.CompilerParams(collective_id=1, has_side_effects=True),
    )(part)


def total_kernel(ns, ng, mine_ref, out_ref, slots, sends, recvs):
    me = lax.axis_index("samp") * ng + lax.axis_index("exp")
    devices = ns * ng
    barrier = pltpu.get_barrier_semaphore()

    def peer_of(k):
        index = lax.rem(me + k, devices)
        return (index // ng, lax.rem(index, ng))

    def hello(k, carry):
        pl.semaphore_signal(barrier, inc=1, device_id=peer_of(k), device_id_type=MESH)
        return carry

    lax.fori_loop(1, devices, hello, 0)
    pl.semaphore_wait(barrier, devices - 1)

    def copy_of(k):
        return remote(mine_ref, slots.at[me], sends.at[k], recvs.at[k], peer_of(k))

    def send(k, carry):
        copy_of(k).start()
        return carry

    lax.fori_loop(1, devices, send, 0)
    slots[me] = mine_ref[...]

    def take(k, carry):
        copy_of(k).wait()
        return carry

    lax.fori_loop(1, devices, take, 0)
    out_ref[...] = jnp.sum(slots[...], axis=0)


def total_of(values, ns, ng):
    devices = ns * ng
    return pl.pallas_call(
        functools.partial(total_kernel, ns, ng),
        out_shape=jax.ShapeDtypeStruct(values.shape, F32),
        in_specs=[VMEM],
        out_specs=VMEM,
        scratch_shapes=[
            pltpu.VMEM((devices,) + values.shape, F32),
            pltpu.SemaphoreType.DMA((devices,)),
            pltpu.SemaphoreType.DMA((devices,)),
        ],
        compiler_params=pltpu.CompilerParams(collective_id=2, has_side_effects=True),
    )(values)


def per_device(
    prompt_states, edit_offsets, targets, router, route_ids, chosen, lengths, w_gate, w_up, w_down
):
    seq = prompt_states.shape[2]
    width = prompt_states.shape[3]
    rounds = route_ids.shape[0]
    top = route_ids.shape[4]
    experts = router.shape[1]
    cap = seq * top * 5 // (4 * experts)
    samplers = lax.axis_size("samp")
    groups = lax.axis_size("exp")
    my_samp = lax.axis_index("samp")
    my_group = lax.axis_index("exp")
    my_expert = my_samp * groups + my_group
    block = -(-groups * cap // 16) * 16
    rows = samplers * block
    tokens = groups * seq
    gate_weight, up_weight, down_weight = w_gate[0], w_up[0], w_down[0]
    meta_width = -(-(experts + 4) // 128) * 128
    expert_iota = jnp.arange(experts, dtype=jnp.int32)
    positions = jnp.arange(seq, dtype=jnp.int32)

    row_iota = jnp.arange(rows, dtype=jnp.int32)
    row_samp = row_iota // block
    row_group = jnp.minimum((row_iota % block) // cap, groups - 1)
    row_repair = row_samp * groups + row_group
    repair_onehot = row_repair[:, None] == jnp.arange(samplers * groups, dtype=jnp.int32)[None, :]
    token_iota = jnp.arange(tokens, dtype=jnp.int32)
    tril = (positions[:, None] <= positions[None, :]).astype(BF16)

    def meta_of(r):
        mask = jnp.any(route_ids[r, 0, 0][:, :, None] == expert_iota[None, None, :], axis=1)
        length = lengths[r, 0, 0]
        cols = jnp.stack(
            [
                positions.astype(BF16),
                (positions < length).astype(BF16),
                jnp.broadcast_to(length.astype(BF16), (seq,)),
                jnp.ones((seq,), BF16),
            ],
            axis=1,
        )
        pad = jnp.zeros((seq, meta_width - experts - 4), BF16)
        return jnp.concatenate([mask.astype(BF16), cols, pad], axis=1)

    def code_of(r):
        hit = metas[r][:, :experts]
        rank = dot_tn(hit, tril) - 1.0
        own = dot_tn(hit, jnp.eye(seq, dtype=BF16))
        code = jnp.where(own > 0.5, rank + (my_group * cap).astype(F32), -1.0)
        return code.reshape(samplers, groups, seq).transpose(1, 0, 2)

    def columns_of(meta):
        info = meta[:, experts : experts + 4].astype(F32)
        used = info[:, 3] > 0.5
        return meta[:, :experts] > 0.5, info[:, 0].astype(jnp.int32), info[:, 1], info[:, 2], used

    def gates_of(received, mask, used):
        logits = dot(received, router)
        sig = jnp.where(mask, jax.nn.sigmoid(logits), 0.0)
        total = jnp.where(used, jnp.sum(sig, axis=1), 1.0)
        own = jnp.sum(jnp.where(expert_iota[None, :] == my_expert, sig, 0.0), axis=1)
        return (own / total).astype(BF16)

    def own_part(x, target, r):
        length = lengths[r, 0, 0]
        valid = (positions < length).astype(F32)
        score = jnp.sum(x.astype(F32) * target.astype(F32), axis=1) / math.sqrt(width)
        return jnp.sum(valid * score) / length.astype(F32)

    def reward_part(hidden, back, gate, valid, length, used, own):
        score = jnp.sum(hidden.astype(F32) * back, axis=1) / math.sqrt(width)
        score = gate.astype(F32) * valid * score / jnp.where(used, length, 1.0)
        part = jnp.sum(jnp.where(repair_onehot, score[:, None], 0.0), axis=0)
        repairs = jnp.arange(samplers * groups, dtype=jnp.int32)
        return part + jnp.where(repairs == my_expert, own, 0.0)

    metas = [meta_of(r) for r in range(rounds)]
    bases = [prompt_states[0, 0]] + [edit_offsets[r, 0, 0] for r in range(rounds - 1)]
    arrays = []
    for r in range(rounds):
        arrays += [jnp.concatenate([bases[r], metas[r]], axis=1), targets[r, 0, 0]]
    code = jnp.concatenate([code_of(r) for r in range(rounds)], axis=2)
    landed = dispatch(code, arrays, samplers, groups, seq, block, rounds)
    parts = []
    saved = []
    mixed = None
    for r in range(rounds):
        arrived, target_rows = landed[2 * r], landed[2 * r + 1]
        mask, row_pos, valid, length, used = columns_of(arrived[:, width:])
        received = arrived[:, :width]
        token_code = jnp.where(used, row_group * seq + row_pos, -1)
        own_x = bases[r]
        if r > 0:
            lift = (token_code[:, None] == token_iota[None, :]).astype(BF16)
            received = (dot(lift, mixed) + received.astype(F32)).astype(BF16)
            best = lax.dynamic_slice_in_dim(mixed, my_group * seq, seq, axis=0)
            own_x = (best.astype(F32) + own_x.astype(F32)).astype(BF16)
        gate = gates_of(received, mask, used)
        pre_gate = dot(received, gate_weight)
        pre_up = dot(received, up_weight)
        hidden = (jax.nn.silu(pre_gate) * pre_up).astype(BF16)
        if r + 1 < rounds:
            choice = chosen[r]
            row_choice = jnp.sum(
                jnp.where(
                    row_group[:, None] == jnp.arange(groups, dtype=jnp.int32)[None, :],
                    choice[None, :],
                    0,
                ),
                axis=1,
            )
            keep = row_samp == row_choice
            slot_code = jnp.where(keep, row_iota % block, -1)
            slots = jnp.arange(block, dtype=jnp.int32)
            take = (slot_code[None, :] == slots[:, None]).astype(BF16)
            result = dot(dot(take, hidden).astype(BF16), down_weight).astype(BF16)
            spread = jnp.where(
                (jnp.where(keep, token_code, -1)[:, None] == token_iota[None, :]),
                gate[:, None],
                jnp.zeros((), BF16),
            )
            combine = dot(take, spread).astype(BF16)
            start = (choice[token_iota // seq] == my_samp) & (token_iota // seq == my_group)
            wide_x = jnp.tile(own_x, (groups, 1)).astype(F32)
            part = dot_tn(combine, result) + jnp.where(start[:, None], wide_x, 0.0)
            mixed = mix(part.astype(BF16), samplers, groups)
        back = dot_nt(target_rows, down_weight)
        parts.append(
            reward_part(
                hidden, back, gate, valid, length, used, own_part(own_x, targets[r, 0, 0], r)
            )
        )
        saved.append((received, target_rows, gate, valid, pre_gate, pre_up, hidden, back))
    filled = jnp.zeros((8, -(-samplers * groups // 128) * 128), F32)
    filled = filled.at[:rounds, : samplers * groups].set(jnp.stack(parts))
    rewards = total_of(filled, samplers, groups)[:rounds, : samplers * groups]
    rewards = rewards.reshape(rounds, samplers, groups)
    advantage = rewards - jnp.mean(rewards, axis=1, keepdims=True)
    flat = advantage.reshape(rounds, samplers * groups)
    grad_gate = grad_up = grad_down = 0.0
    for r, (received, target_rows, gate, valid, pre_gate, pre_up, hidden, back) in enumerate(saved):
        row_adv = jnp.sum(jnp.where(repair_onehot, flat[r][None, :], 0.0), axis=1)
        coef = (row_adv * valid * gate.astype(F32)).astype(BF16).astype(F32)[:, None]
        hidden_grad = coef * back
        sg = jax.nn.sigmoid(pre_gate)
        gate_grad = (hidden_grad * pre_up * sg * (1.0 + pre_gate * (1.0 - sg))).astype(BF16)
        up_grad = (hidden_grad * pre_gate * sg).astype(BF16)
        weighted = (hidden.astype(F32) * coef).astype(BF16)
        grad_down = grad_down + dot_tn(weighted, target_rows)
        grad_gate = grad_gate + dot_tn(received, gate_grad)
        grad_up = grad_up + dot_tn(received, up_grad)
    repairs = jnp.arange(samplers * groups, dtype=jnp.int32)
    my_adv = jnp.sum(jnp.where(repairs[None, :] == my_expert, flat, 0.0), axis=1)
    return (
        grad_gate.astype(BF16)[None],
        grad_up.astype(BF16)[None],
        grad_down.astype(BF16)[None],
        my_adv.reshape(rounds, 1, 1),
    )


def solution(mesh):
    placed = (
        P("exp", "samp", None, None),
        P(None, "exp", "samp", None, None),
        P(None, "exp", "samp", None, None),
        P(),
        P(None, "exp", "samp", None, None),
        P(),
        P(None, "exp", "samp"),
        P(("samp", "exp"), None, None),
        P(("samp", "exp"), None, None),
        P(("samp", "exp"), None, None),
    )
    return jax.shard_map(
        per_device,
        mesh=mesh,
        in_specs=placed,
        out_specs=(
            P(("samp", "exp"), None, None),
            P(("samp", "exp"), None, None),
            P(("samp", "exp"), None, None),
            P(None, "exp", "samp"),
        ),
        check_vma=False,
    )
```

```python
import functools
import math

import jax
import jax.numpy as jnp
from jax import lax
from jax.experimental import pallas as pl
from jax.experimental.pallas import tpu as pltpu
from jax.sharding import PartitionSpec as P

F32 = jnp.float32
BF16 = jnp.bfloat16


def dot(a, b):
    return jnp.dot(a, b, preferred_element_type=F32)


def dot_tn(a, b):
    return lax.dot_general(a, b, (((0,), (0,)), ((), ())), preferred_element_type=F32)


def dot_nt(a, b):
    return lax.dot_general(a, b, (((1,), (1,)), ((), ())), preferred_element_type=F32)


MESH = pl.DeviceIdType.MESH
VMEM = pl.BlockSpec(memory_space=pltpu.VMEM)
ANY = pl.BlockSpec(memory_space=pl.ANY)


def greet(peers):
    barrier = pltpu.get_barrier_semaphore()
    for peer in peers:
        pl.semaphore_signal(barrier, inc=1, device_id=peer, device_id_type=MESH)
    pl.semaphore_wait(barrier, len(peers))


def remote(src, dst, send, recv, peer):
    return pltpu.make_async_remote_copy(
        src_ref=src, dst_ref=dst, send_sem=send, recv_sem=recv, device_id=peer, device_id_type=MESH
    )


def dispatch_kernel(ns, ng, seq, block, rounds, chunks, *refs):
    count = 2 * rounds
    code_ref, meta_ref, target_ref = refs[:3]
    bases = refs[3 : 3 + rounds]
    outs, rest = refs[3 + rounds : 3 + rounds + count], refs[3 + rounds + count :]
    codes, alls, sends = rest[0], rest[1 : 1 + count], list(rest[1 + count : count * 2]) + [outs[-1]]
    place, gs, gr, ss, sr, own_sem = rest[count * 2 :]
    width = bases[0].shape[1]
    me_s, me_g = lax.axis_index("samp"), lax.axis_index("exp")
    exp_peers = [(me_s, lax.rem(me_g + k, ng)) for k in range(1, ng)]
    samp_peers = [(lax.rem(me_s + k, ns), me_g) for k in range(1, ns)]
    mine = pl.ds(pl.multiple_of(me_g * seq, seq), seq)
    codes[me_g] = code_ref[me_g]
    for r in range(rounds):
        alls[r][mine, :width] = bases[r][...]
        alls[r][mine, width:] = meta_ref[r]
        alls[rounds + r][mine, :] = target_ref[r]
    greet(exp_peers + samp_peers)

    def gather(j):
        i, lo, hi = chunks[j]
        part = alls[i].at[mine, lo:hi]
        here = [remote(part, part, gs.at[j, k], gr.at[j, k], p) for k, p in enumerate(exp_peers)]
        for copy in here:
            copy.start()
        return here

    code_copies = []
    for k, peer in enumerate(exp_peers):
        at = len(chunks)
        copy = remote(code_ref.at[peer[1]], codes.at[me_g], gs.at[at, k], gr.at[at, k], peer)
        copy.start()
        code_copies.append(copy)
    flying = gather(0)
    for copy in code_copies:
        copy.wait()
    slots = lax.broadcasted_iota(jnp.int32, (block, ng * seq), 0).astype(F32)
    for r in range(rounds):
        line = jnp.concatenate([codes[g][:, r * seq : (r + 1) * seq] for g in range(ng)], axis=1)
        for d in range(ns):
            hit = jnp.where(line[d : d + 1, :] == slots, 1.0, 0.0)
            place[r, d * block : (d + 1) * block, :] = hit.astype(BF16)
    home = pl.ds(pl.multiple_of(me_s * block, block), block)

    def rows_of(d):
        return pl.ds(pl.multiple_of(d * block, block), block)

    def plane_copy(j, k):
        i, lo, hi = chunks[j]
        d = lax.rem(me_s + k, ns)
        src, dst = sends[i].at[rows_of(d), lo:hi], outs[i].at[home, lo:hi]
        return remote(src, dst, ss.at[j, k], sr.at[j, k], (d, me_g))

    def home_copy(j):
        i, lo, hi = chunks[j]
        return pltpu.make_async_copy(
            sends[i].at[home, lo:hi], outs[i].at[home, lo:hi], own_sem.at[j]
        )

    for j, (i, lo, hi) in enumerate(chunks):
        for copy in flying:
            copy.wait()
        if j + 1 < len(chunks):
            flying = gather(j + 1)
        held = i == count - 1

        def step(k, carry, j=j, i=i, lo=lo, hi=hi, held=held):
            d = lax.rem(me_s + k, ns)
            placed = dot(place[i % rounds, rows_of(d), :], alls[i][:, lo:hi])
            sends[i][rows_of(d), lo:hi] = placed.astype(BF16)
            if not held:
                plane_copy(j, k).start()
            return carry

        lax.fori_loop(1, ns, step, 0)
        placed = dot(place[i % rounds, home, :], alls[i][:, lo:hi])
        sends[i][home, lo:hi] = placed.astype(BF16)
        if not held:
            home_copy(j).start()
    for j, (i, lo, hi) in enumerate(chunks):
        if i == count - 1:
            continue

        def finish(k, carry, j=j):
            plane_copy(j, k).wait()
            return carry

        lax.fori_loop(1, ns, finish, 0)
        home_copy(j).wait()


def dispatch(code, metas, targets, bases, ns, ng, seq, block, rounds):
    width, extra = bases[0].shape[1], metas.shape[2]
    widths = [width + extra] * rounds + [width] * rounds
    half = width // 2
    chunks = [(0, 0, half), (0, half, widths[0])] + [
        (i, 0, widths[i]) for i in range(1, 2 * rounds)
    ]
    steps = len(chunks)
    return pl.pallas_call(
        functools.partial(dispatch_kernel, ns, ng, seq, block, rounds, chunks),
        out_shape=[jax.ShapeDtypeStruct((ns * block, w), BF16) for w in widths],
        in_specs=[VMEM] * (3 + rounds),
        out_specs=[ANY] * (2 * rounds - 1) + [VMEM],
        scratch_shapes=[pltpu.VMEM(code.shape, F32)]
        + [pltpu.VMEM((ng * seq, w), BF16) for w in widths]
        + [pltpu.VMEM((ns * block, w), BF16) for w in widths[:-1]]
        + [
            pltpu.VMEM((rounds, ns * block, ng * seq), BF16),
            pltpu.SemaphoreType.DMA((steps + 1, ng - 1)),
            pltpu.SemaphoreType.DMA((steps + 1, ng - 1)),
            pltpu.SemaphoreType.DMA((steps, ns)),
            pltpu.SemaphoreType.DMA((steps, ns)),
            pltpu.SemaphoreType.DMA((steps,)),
        ],
        compiler_params=pltpu.CompilerParams(
            collective_id=0, has_side_effects=True, vmem_limit_bytes=48 * 2**20
        ),
    )(code, metas, targets, *bases)


def mix_kernel(
    ns, ng, part_ref, ahead_ref, out_ref, landed_ref, rows_in, half, cols_in, final, sems_a, sems_b, own
):
    me_s, me_g = lax.axis_index("samp"), lax.axis_index("exp")
    exp_peers = [(me_s, lax.rem(me_g + k, ng)) for k in range(1, ng)]
    samp_peers = [(lax.rem(me_s + k, ns), me_g) for k in range(1, ns)]
    greet(exp_peers + samp_peers)
    high, width = rows_in.shape[1], rows_in.shape[2]
    wide = width // ng

    def rows_of(d):
        return pl.ds(pl.multiple_of(d * high, high), high)

    def cols_of(g):
        return pl.ds(pl.multiple_of(g * wide, wide), wide)

    copies = []
    for k, peer in enumerate(samp_peers):
        copy = remote(
            part_ref.at[rows_of(peer[0]), :],
            rows_in.at[k],
            sems_a.at[0, k],
            sems_a.at[1, k],
            peer,
        )
        copy.start()
        copies.append(copy)
    half[...] = part_ref[rows_of(me_s), :].astype(F32)
    for k, copy in enumerate(copies):
        copy.wait()
        half[...] += rows_in[k].astype(F32)
    block = ahead_ref.shape[0] // ns

    def block_of(d):
        return pl.ds(pl.multiple_of(d * block, block), block)

    ahead = [
        remote(
            ahead_ref.at[block_of(peer[0]), :],
            landed_ref.at[block_of(me_s), :],
            sems_a.at[4, k],
            sems_a.at[5, k],
            peer,
        )
        for k, peer in enumerate(samp_peers)
    ]
    ahead.append(
        pltpu.make_async_copy(
            ahead_ref.at[block_of(me_s), :], landed_ref.at[block_of(me_s), :], own
        )
    )
    copies = []
    for k, peer in enumerate(exp_peers):
        copy = remote(
            half.at[:, cols_of(peer[1])], cols_in.at[k], sems_b.at[0, k], sems_b.at[1, k], peer
        )
        copy.start()
        copies.append(copy)
    for copy in ahead:
        copy.start()
    total = half[:, cols_of(me_g)]
    for k, copy in enumerate(copies):
        copy.wait()
        total = total + cols_in[k]
    final[...] = total.astype(BF16)
    out_ref[rows_of(me_s), cols_of(me_g)] = final[...]
    copies = []
    for k, peer in enumerate(exp_peers):
        copy = remote(
            final,
            out_ref.at[rows_of(me_s), cols_of(me_g)],
            sems_b.at[2, k],
            sems_b.at[3, k],
            peer,
        )
        copy.start()
        copies.append(copy)
    for copy in copies:
        copy.wait()
    copies = []
    for k, peer in enumerate(samp_peers):
        copy = remote(
            out_ref.at[rows_of(me_s), :],
            out_ref.at[rows_of(me_s), :],
            sems_a.at[2, k],
            sems_a.at[3, k],
            peer,
        )
        copy.start()
        copies.append(copy)
    for copy in copies + ahead:
        copy.wait()


def mix(part, ahead, ns, ng):
    tokens, width = part.shape
    high = tokens // ns
    return pl.pallas_call(
        functools.partial(mix_kernel, ns, ng),
        out_shape=[
            jax.ShapeDtypeStruct(part.shape, BF16),
            jax.ShapeDtypeStruct(ahead.shape, BF16),
        ],
        in_specs=[VMEM, ANY],
        out_specs=[VMEM, ANY],
        scratch_shapes=[
            pltpu.VMEM((ns - 1, high, width), BF16),
            pltpu.VMEM((high, width), F32),
            pltpu.VMEM((ng - 1, high, width // ng), F32),
            pltpu.VMEM((high, width // ng), BF16),
            pltpu.SemaphoreType.DMA((6, ns - 1)),
            pltpu.SemaphoreType.DMA((4, ng - 1)),
            pltpu.SemaphoreType.DMA,
        ],
        compiler_params=pltpu.CompilerParams(collective_id=1, has_side_effects=True),
    )(part, ahead)


def total_kernel(ns, ng, mine_ref, out_ref, slots, sends, recvs):
    me = lax.axis_index("samp") * ng + lax.axis_index("exp")
    devices = ns * ng
    barrier = pltpu.get_barrier_semaphore()

    def peer_of(k):
        index = lax.rem(me + k, devices)
        return (index // ng, lax.rem(index, ng))

    def hello(k, carry):
        pl.semaphore_signal(barrier, inc=1, device_id=peer_of(k), device_id_type=MESH)
        return carry

    lax.fori_loop(1, devices, hello, 0)
    pl.semaphore_wait(barrier, devices - 1)

    def copy_of(k):
        return remote(mine_ref, slots.at[me], sends.at[k], recvs.at[k], peer_of(k))

    def send(k, carry):
        copy_of(k).start()
        return carry

    lax.fori_loop(1, devices, send, 0)
    slots[me] = mine_ref[...]

    def take(k, carry):
        copy_of(k).wait()
        return carry

    lax.fori_loop(1, devices, take, 0)
    out_ref[...] = jnp.sum(slots[...], axis=0)


def total_of(values, ns, ng):
    devices = ns * ng
    return pl.pallas_call(
        functools.partial(total_kernel, ns, ng),
        out_shape=jax.ShapeDtypeStruct(values.shape, F32),
        in_specs=[VMEM],
        out_specs=VMEM,
        scratch_shapes=[
            pltpu.VMEM((devices,) + values.shape, F32),
            pltpu.SemaphoreType.DMA((devices,)),
            pltpu.SemaphoreType.DMA((devices,)),
        ],
        compiler_params=pltpu.CompilerParams(collective_id=2, has_side_effects=True),
    )(values)


def per_device(
    prompt_states, edit_offsets, targets, router, route_ids, chosen, lengths, w_gate, w_up, w_down
):
    seq = prompt_states.shape[2]
    width = prompt_states.shape[3]
    rounds = route_ids.shape[0]
    top = route_ids.shape[4]
    experts = router.shape[1]
    cap = seq * top * 5 // (4 * experts)
    samplers = lax.axis_size("samp")
    groups = lax.axis_size("exp")
    my_samp = lax.axis_index("samp")
    my_group = lax.axis_index("exp")
    my_expert = my_samp * groups + my_group
    block = -(-groups * cap // 16) * 16
    rows = samplers * block
    tokens = groups * seq
    gate_weight, up_weight, down_weight = w_gate[0], w_up[0], w_down[0]
    meta_width = -(-(experts + 4) // 128) * 128
    expert_iota = jnp.arange(experts, dtype=jnp.int32)
    positions = jnp.arange(seq, dtype=jnp.int32)

    row_iota = jnp.arange(rows, dtype=jnp.int32)
    row_samp = row_iota // block
    row_group = jnp.minimum((row_iota % block) // cap, groups - 1)
    row_repair = row_samp * groups + row_group
    repair_onehot = row_repair[:, None] == jnp.arange(samplers * groups, dtype=jnp.int32)[None, :]
    token_iota = jnp.arange(tokens, dtype=jnp.int32)
    tril = (positions[:, None] <= positions[None, :]).astype(BF16)

    def meta_of(r):
        mask = jnp.any(route_ids[r, 0, 0][:, :, None] == expert_iota[None, None, :], axis=1)
        length = lengths[r, 0, 0]
        cols = jnp.stack(
            [
                positions.astype(BF16),
                (positions < length).astype(BF16),
                jnp.broadcast_to(length.astype(BF16), (seq,)),
                jnp.ones((seq,), BF16),
            ],
            axis=1,
        )
        pad = jnp.zeros((seq, meta_width - experts - 4), BF16)
        return jnp.concatenate([mask.astype(BF16), cols, pad], axis=1)

    def code_of(r):
        hit = metas[r][:, :experts]
        rank = dot_tn(hit, tril) - 1.0
        own = dot_tn(hit, jnp.eye(seq, dtype=BF16))
        code = jnp.where(own > 0.5, rank + (my_group * cap).astype(F32), -1.0)
        return code.reshape(samplers, groups, seq).transpose(1, 0, 2)

    def columns_of(meta):
        info = meta[:, experts : experts + 4].astype(F32)
        used = info[:, 3] > 0.5
        return meta[:, :experts] > 0.5, info[:, 0].astype(jnp.int32), info[:, 1], info[:, 2], used

    def gates_of(received, mask, used):
        logits = dot(received, router)
        sig = jnp.where(mask, jax.nn.sigmoid(logits), 0.0)
        total = jnp.where(used, jnp.sum(sig, axis=1), 1.0)
        own = jnp.sum(jnp.where(expert_iota[None, :] == my_expert, sig, 0.0), axis=1)
        return (own / total).astype(BF16)

    def own_part(x, target, r):
        length = lengths[r, 0, 0]
        valid = (positions < length).astype(F32)
        score = jnp.sum(x.astype(F32) * target.astype(F32), axis=1) / math.sqrt(width)
        return jnp.sum(valid * score) / length.astype(F32)

    def reward_part(hidden, back, gate, valid, length, used, own):
        score = jnp.sum(hidden.astype(F32) * back, axis=1) / math.sqrt(width)
        score = gate.astype(F32) * valid * score / jnp.where(used, length, 1.0)
        part = jnp.sum(jnp.where(repair_onehot, score[:, None], 0.0), axis=0)
        repairs = jnp.arange(samplers * groups, dtype=jnp.int32)
        return part + jnp.where(repairs == my_expert, own, 0.0)

    metas = [meta_of(r) for r in range(rounds)]
    bases = [prompt_states[0, 0]] + [edit_offsets[r, 0, 0] for r in range(rounds - 1)]
    code = jnp.concatenate([code_of(r) for r in range(rounds)], axis=2)
    landed = list(
        dispatch(
            code, jnp.stack(metas), targets[:, 0, 0], bases, samplers, groups, seq, block, rounds
        )
    )
    parts = []
    saved = []
    mixed = None
    for r in range(rounds):
        arrived, target_rows = landed[r], landed[rounds + r]
        mask, row_pos, valid, length, used = columns_of(arrived[:, width:])
        received = arrived[:, :width]
        token_code = jnp.where(used, row_group * seq + row_pos, -1)
        own_x = bases[r]
        if r > 0:
            lift = (token_code[:, None] == token_iota[None, :]).astype(BF16)
            received = (dot(lift, mixed) + received.astype(F32)).astype(BF16)
            best = lax.dynamic_slice_in_dim(mixed, my_group * seq, seq, axis=0)
            own_x = (best.astype(F32) + own_x.astype(F32)).astype(BF16)
        gate = gates_of(received, mask, used)
        pre_gate = dot(received, gate_weight)
        pre_up = dot(received, up_weight)
        hidden = (jax.nn.silu(pre_gate) * pre_up).astype(BF16)
        if r + 1 < rounds:
            choice = chosen[r]
            row_choice = jnp.sum(
                jnp.where(
                    row_group[:, None] == jnp.arange(groups, dtype=jnp.int32)[None, :],
                    choice[None, :],
                    0,
                ),
                axis=1,
            )
            keep = row_samp == row_choice
            slot_code = jnp.where(keep, row_iota % block, -1)
            slots = jnp.arange(block, dtype=jnp.int32)
            take = (slot_code[None, :] == slots[:, None]).astype(BF16)
            result = dot(dot(take, hidden).astype(BF16), down_weight).astype(BF16)
            spread = jnp.where(
                (jnp.where(keep, token_code, -1)[:, None] == token_iota[None, :]),
                gate[:, None],
                jnp.zeros((), BF16),
            )
            combine = dot(take, spread).astype(BF16)
            start = (choice[token_iota // seq] == my_samp) & (token_iota // seq == my_group)
            wide_x = jnp.tile(own_x, (groups, 1)).astype(F32)
            part = dot_tn(combine, result) + jnp.where(start[:, None], wide_x, 0.0)
            mixed, landed[-1] = mix(part.astype(BF16), landed[-1], samplers, groups)
        back = dot_nt(target_rows, down_weight)
        parts.append(
            reward_part(
                hidden, back, gate, valid, length, used, own_part(own_x, targets[r, 0, 0], r)
            )
        )
        saved.append((received, target_rows, gate, valid, pre_gate, pre_up, hidden, back))
    filled = jnp.zeros((8, -(-samplers * groups // 128) * 128), F32)
    filled = filled.at[:rounds, : samplers * groups].set(jnp.stack(parts))
    rewards = total_of(filled, samplers, groups)[:rounds, : samplers * groups]
    rewards = rewards.reshape(rounds, samplers, groups)
    advantage = rewards - jnp.mean(rewards, axis=1, keepdims=True)
    flat = advantage.reshape(rounds, samplers * groups)
    grad_gate = grad_up = grad_down = 0.0
    for r, (received, target_rows, gate, valid, pre_gate, pre_up, hidden, back) in enumerate(saved):
        row_adv = jnp.sum(jnp.where(repair_onehot, flat[r][None, :], 0.0), axis=1)
        coef = (row_adv * valid * gate.astype(F32)).astype(BF16).astype(F32)[:, None]
        hidden_grad = coef * back
        sg = jax.nn.sigmoid(pre_gate)
        gate_grad = (hidden_grad * pre_up * sg * (1.0 + pre_gate * (1.0 - sg))).astype(BF16)
        up_grad = (hidden_grad * pre_gate * sg).astype(BF16)
        weighted = (hidden.astype(F32) * coef).astype(BF16)
        grad_down = grad_down + dot_tn(weighted, target_rows)
        grad_gate = grad_gate + dot_tn(received, gate_grad)
        grad_up = grad_up + dot_tn(received, up_grad)
    repairs = jnp.arange(samplers * groups, dtype=jnp.int32)
    my_adv = jnp.sum(jnp.where(repairs[None, :] == my_expert, flat, 0.0), axis=1)
    return (
        grad_gate.astype(BF16)[None],
        grad_up.astype(BF16)[None],
        grad_down.astype(BF16)[None],
        my_adv.reshape(rounds, 1, 1),
    )


def solution(mesh):
    placed = (
        P("exp", "samp", None, None),
        P(None, "exp", "samp", None, None),
        P(None, "exp", "samp", None, None),
        P(),
        P(None, "exp", "samp", None, None),
        P(),
        P(None, "exp", "samp"),
        P(("samp", "exp"), None, None),
        P(("samp", "exp"), None, None),
        P(("samp", "exp"), None, None),
    )
    return jax.shard_map(
        per_device,
        mesh=mesh,
        in_specs=placed,
        out_specs=(
            P(("samp", "exp"), None, None),
            P(("samp", "exp"), None, None),
            P(("samp", "exp"), None, None),
            P(None, "exp", "samp"),
        ),
        check_vma=False,
    )
```
